512 devices in a mesh: user: 8 (over z), item: 4 (over x), tm: 16 (over y, core).
Axes of the slice: x: 4, y: 8, z: 8, core: 2. Of those that a mesh axis runs over, the one named last changes fastest.
Arguments:
- blocks: bfloat16 [8, 4, 16, 8, 64, 4096], P('user', 'item', 'tm'), may hold values from 0 to 8
- block_coords: int32 [8, 4, 16, 8, 3], P('user', 'item', 'tm'), may hold values from 0 to 127, as said below
- block_count: int32 [8, 4, 16], P('user', 'item', 'tm'), may hold values from 1 to 8, as said below
- a_factor: float32 [8192, 128], P(('user', 'item', 'tm')), as said below
- item_factor: bfloat16 [4096, 128], P(('item', 'user', 'tm')), as said below
- hour_factor: bfloat16 [8192, 128], P(('tm', 'user', 'item')), as said below
Outputs:
- new_factor: float32 [8192, 128], P(('user', 'item', 'tm'))
The draws below stay inside these ranges and needn't reach their ends.
Inputs may be any that keep to these rules, and one draw needn't show every extreme that they name: `block_coords`: the user block of a slot of device (u, i, t) lies in u * 16 to u * 16 + 15, its item block in i * 16 to i * 16 + 15, its hour block in t * 8 to t * 8 + 7; the 8 slots of a device name distinct blocks; slots at or past the device's count are not part of the tensor. `block_count`: some device lists all 8 slots. `a_factor`: entries are nonnegative. `item_factor`: entries are positive. `hour_factor`: entries are positive.
All inputs are finite; a program needn't handle non-finite values.
Results may differ from the reference program's by a relative error of at most 0.00045.
Values may be sent and summed in bfloat16 or wider, within the bound.
A program may use at most 64 MiB of HBM per device.

```python
import math
import jax
import jax.numpy as jnp
from jax import lax

BS = 64
R = 128
UB = 16
IB = 16
HB = 8
NB = 8
USERS = 8192
ITEMS = 4096
HOURS = 8192
N_USER = 8
N_ITEM = 4
N_TM = 16


shrink_factor = 0.1


def factor_values(key, rows, cols):
    first, second = jax.random.split(key, 2)
    scale = jnp.exp(jax.random.uniform(first, (rows, 1), jnp.float32) * math.log(10.0))
    base = jax.random.uniform(second, (rows, cols), jnp.float32, 0.05, 1.0)
    ramp = 1.0 + 2.0 * jnp.arange(rows, dtype=jnp.float32) / (rows - 1)
    return (shrink_factor * scale * ramp[:, None] * base / math.sqrt(rows)).astype(jnp.bfloat16)


def draw_item_factor(key, part):
    return factor_values(key, ITEMS, R)


def draw_hour_factor(key, part):
    return factor_values(key, HOURS, R)


def fit_level():
    light_mean = (NB // 4 + 2) / 2.0
    per_block = N_ITEM * N_TM * (0.25 * NB + 0.75 * light_mean) / UB
    top = 10.0
    base_mean = 0.525
    base_square = 0.2756
    mean_scale = (top - 1.0) / math.log(top)
    square_scale = (top * top - 1.0) / (2.0 * math.log(top))
    factor_mean = shrink_factor * mean_scale * 2.0 * base_mean
    target = 4.0 * BS * BS * factor_mean * factor_mean / math.sqrt(ITEMS * HOURS) * per_block
    single = shrink_factor * shrink_factor * square_scale * (13.0 / 3.0) * base_square
    return target / ((R + 0.5) * single * single)


def draw_a_factor(key, part):
    level = fit_level()
    first = jax.random.fold_in(key, 0)
    values = jax.random.uniform(first, (USERS, R), jnp.float32, 0.0, 1.6) * level
    return values.astype(jnp.float32)


def draw_block_count(key, part):
    shape = (N_USER, N_ITEM, N_TM)
    first, second, third = jax.random.split(key, 3)
    heavy = jax.random.randint(first, shape, 0, 4) == 0
    light = jax.random.randint(second, shape, 1, NB // 4 + 2)
    chosen = jax.random.randint(third, (), 0, N_USER * N_ITEM * N_TM)
    flat = jnp.arange(N_USER * N_ITEM * N_TM, dtype=jnp.int32).reshape(shape)
    return jnp.where(heavy | (flat == chosen), NB, light).astype(jnp.int32)


def device_picks(one):
    cells = UB * IB * HB
    first, second = jax.random.split(one)
    rest = jax.random.permutation(first, cells - 2)[:NB - 2].astype(jnp.int32) + 1
    ends = jnp.array([cells - 1, 0], dtype=jnp.int32)
    chosen = jnp.concatenate([ends, rest])
    order = jax.random.permutation(second, NB).astype(jnp.int32)
    return jnp.take(chosen, order)


def draw_block_coords(key, part):
    devices = N_USER * N_ITEM * N_TM
    keys = jax.random.split(key, devices)
    picks = jax.vmap(device_picks)(keys)
    user_block = picks // (IB * HB)
    item_block = picks // HB % IB
    hour_block = picks % HB
    device = jnp.arange(devices, dtype=jnp.int32)
    user_dev = device // (N_ITEM * N_TM)
    item_dev = device // N_TM % N_ITEM
    hour_dev = device % N_TM
    stacked = jnp.stack([user_block + user_dev[:, None] * UB, item_block + item_dev[:, None] * IB, hour_block + hour_dev[:, None] * HB], axis=-1)
    return stacked.reshape(N_USER, N_ITEM, N_TM, NB, 3).astype(jnp.int32)


def block_levels(rng, extent, pieces, smallest, largest):
    def one(dim, parts):
        heights = jax.random.uniform(jax.random.fold_in(jax.random.fold_in(rng, 6), dim), (parts,), jnp.float32, smallest / len(pieces), largest / len(pieces))
        return jnp.repeat(jnp.exp(heights), extent[dim] // parts).reshape((-1,) + (1,) * (len(extent) - dim - 1))

    level = one(*pieces[0])
    for cut in pieces[1:]:
        level = level * one(*cut)
    return level


def setup_inputs(seed: int = 0) -> dict:
    key_of = jax.random.split(jax.random.key(seed), 7)
    blocks = jnp.clip(8.0 * jax.random.uniform(key_of[0], (N_USER, N_ITEM, N_TM, NB, BS, BS * BS), jnp.float32) ** block_levels(key_of[0], (N_USER, N_ITEM, N_TM, NB, BS, BS * BS), ((0, 8), (1, 4), (2, 16)), -0.2, 0.2), 0.0, 8.0).astype(jnp.bfloat16)
    block_coords = draw_block_coords(jax.random.fold_in(key_of[6], 71), 0)
    block_count = draw_block_count(jax.random.fold_in(key_of[6], 71), 0)
    a_factor = draw_a_factor(jax.random.fold_in(key_of[6], 71), 0)
    item_factor = draw_item_factor(jax.random.fold_in(key_of[6], 71), 0)
    hour_factor = draw_hour_factor(jax.random.fold_in(key_of[6], 71), 0)
    return {"blocks": blocks, "block_coords": block_coords, "block_count": block_count, "a_factor": a_factor, "item_factor": item_factor, "hour_factor": hour_factor}


def update_column(factor, mttkrp, gram, column):
    weights = lax.dynamic_index_in_dim(gram, column, 1, keepdims=False)
    pivot = lax.dynamic_index_in_dim(weights, column, 0, keepdims=False)
    current = lax.dynamic_index_in_dim(factor, column, 1, keepdims=False)
    target = lax.dynamic_index_in_dim(mttkrp, column, 1, keepdims=False)
    fitted = jnp.dot(factor, weights, precision=lax.Precision.HIGHEST)
    fresh = jnp.maximum(current + (target - fitted) / pivot, 0.0)
    return lax.dynamic_update_index_in_dim(factor, fresh, column, 1)


def self_product(matrix):
    return lax.dot_general(matrix, matrix, (((0,), (0,)), ((), ())), preferred_element_type=jnp.float32)


def reference(blocks, block_coords, block_count, a_factor, item_factor, hour_factor):
    tiles = blocks.reshape(-1, BS, BS * BS)
    coords = block_coords.reshape(-1, 3)
    listed = (jnp.arange(NB, dtype=jnp.int32)[None, None, None, :] < block_count[..., None]).reshape(-1)

    def step(totals, item):
        tile, coord, flag = item
        item_rows = lax.dynamic_slice_in_dim(item_factor, (coord[1] * BS).astype(jnp.int32), BS, 0).astype(jnp.float32)
        hour_rows = lax.dynamic_slice_in_dim(hour_factor, (coord[2] * BS).astype(jnp.int32), BS, 0).astype(jnp.float32)
        khatri = (item_rows[:, None, :] * hour_rows[None, :, :]).reshape(BS * BS, R).astype(jnp.bfloat16)
        term = jnp.dot(tile, khatri, preferred_element_type=jnp.float32) * flag.astype(jnp.float32)
        start = (coord[0] * BS).astype(jnp.int32)
        current = lax.dynamic_slice_in_dim(totals, start, BS, 0)
        return lax.dynamic_update_slice_in_dim(totals, current + term, start, 0), None

    mttkrp, _ = lax.scan(step, jnp.zeros((USERS, R), jnp.float32), (tiles, coords, listed))
    gram = self_product(item_factor) * self_product(hour_factor)

    def sweep(column, factor):
        return update_column(factor, mttkrp, gram, column)

    return lax.fori_loop(0, R, sweep, a_factor)
```

```python
import functools

import jax
import jax.numpy as jnp
from jax import lax
from jax.experimental import pallas as pl
from jax.experimental.pallas import tpu as pltpu
from jax.sharding import PartitionSpec as P

F32 = jnp.float32
BF16 = jnp.bfloat16
RANK_TILE = 8


def nearest_first(n):
    return sorted(range(1, n), key=lambda d: (min(d, n - d), d))


def farthest_first(n):
    return sorted(range(1, n), key=lambda d: (-min(d, n - d), d))


def self_product(rows):
    return lax.dot_general(rows, rows, (((0,), (0,)), ((), ())), preferred_element_type=F32)


def exchange_kernel(
    nu, ni, nt,
    coords, count, blocks, item, hour,
    mttkrp_out, gram_out,
    items, hours, tiles, terms, totals, from_core, from_x, mine_x, from_y,
    gram_i, gram_h, strip_core, strip_h, strip_y, strip_x, strip, gram,
    tile_sem, z_send, z_recv, zh_send, zh_recv, y_send, y_recv, c_send, c_recv, x_send, x_recv,
    g_send, g_recv, gy_send, gy_recv, gx_send, gx_recv, gz_send, gz_recv,
    rc_send, rc_recv, rx_send, rx_recv, ry_send, ry_recv,
):
    ny = nt // 2
    u = lax.axis_index("user")
    i = lax.axis_index("item")
    t = lax.axis_index("tm")
    y, c = t // 2, t % 2
    slots, width, _ = tiles.shape
    ri, rh = item.shape[0], hour.shape[0]
    rank = item.shape[1]
    share = mttkrp_out.shape[0]
    strip_rows = strip.shape[0]

    def at_user(d):
        return {"user": (u + d) % nu}

    def at_item(d):
        return {"item": (i + d) % ni}

    def at_y(d):
        return {"tm": ((y + d) % ny) * 2 + c}

    sibling = {"tm": y * 2 + 1 - c}

    def remote(src, dst, send, recv, device):
        return pltpu.make_async_remote_copy(
            src_ref=src, dst_ref=dst, send_sem=send, recv_sem=recv,
            device_id=device, device_id_type=pl.DeviceIdType.MESH,
        )

    def tile_copy(s):
        return pltpu.make_async_copy(blocks.at[s], tiles.at[s], tile_sem.at[s])

    for s in range(slots):
        tile_copy(s).start()

    barrier = pltpu.get_barrier_semaphore()
    partners = (
        [at_user(d) for d in range(1, nu)]
        + [at_item(d) for d in range(1, ni)]
        + [at_y(d) for d in range(1, ny)]
        + [sibling]
    )
    for device in partners:
        pl.semaphore_signal(barrier, inc=1, device_id=device, device_id_type=pl.DeviceIdType.MESH)
    items[t, u] = item[...]
    hours[i, u] = hour[...]
    pl.semaphore_wait(barrier, len(partners))

    sent = []

    def start(copy):
        copy.start()
        sent.append(copy)
        return copy

    z_copies = []
    for d in farthest_first(nu):
        z_copies.append(start(remote(hour, hours.at[i, u], zh_send.at[d], zh_recv.at[d], at_user(d))))
        z_copies.append(start(remote(item, items.at[t, u], z_send.at[d], z_recv.at[d], at_user(d))))
    for copy in z_copies:
        copy.wait_recv()

    y_copies = {}
    for d in farthest_first(ny):
        y_copies[d] = start(remote(items.at[t], items.at[t], y_send.at[d], y_recv.at[d], at_y(d)))
    x_copies = []
    for d in farthest_first(ni):
        x_copies.append(start(remote(hours.at[i], hours.at[i], x_send.at[d], x_recv.at[d], at_item(d))))
    c_copies = [start(remote(items.at[t], items.at[t], c_send.at[0], c_recv.at[0], sibling))]
    for d in nearest_first(ny):
        y_copies[d].wait_recv()
        source = ((y + ny - d) % ny) * 2 + c
        c_copies.append(
            start(remote(items.at[source], items.at[source], c_send.at[d], c_recv.at[d], sibling))
        )
    for copy in x_copies:
        copy.wait_recv()

    own_strip = pl.ds(pl.multiple_of(u * strip_rows, strip_rows), strip_rows)
    gram_h[...] = self_product(hours[...].reshape(ni * nu * rh, rank))
    g_copy = start(remote(gram_h.at[own_strip], strip_core, g_send, g_recv, sibling))
    for copy in c_copies:
        copy.wait_recv()
    gram_i[...] = self_product(items[...].reshape(nt * nu * ri, rank))
    gx_copies = [
        start(remote(gram_i.at[own_strip], strip_x.at[d], gx_send.at[d], gx_recv.at[d], at_item(d)))
        for d in farthest_first(ni)
    ]

    user_blocks = (share * ni * nt) // width
    item_blocks = (ri * nu * nt) // width
    hour_blocks = (rh * nu * ni) // width
    span = width // ri
    per_user = nt // span

    def products(low, high):
        @pl.loop(low, high)
        def _(s):
            tile_copy(s).wait()
            item_block = lax.rem(coords[s, 1], item_blocks)
            hour_block = lax.rem(coords[s, 2], hour_blocks)
            item_rows = (
                items[pl.ds(lax.rem(item_block, per_user) * span, span), lax.div(item_block, per_user)]
                .astype(F32)
                .reshape(width, rank)
            )
            hour_rows = hours[:, hour_block].astype(F32).reshape(width, rank)
            group = 16
            term = jnp.zeros((width, rank), F32)
            for g in range(width // group):
                khatri = jnp.concatenate(
                    [
                        (item_rows[j : j + 1, :] * hour_rows).astype(BF16)
                        for j in range(g * group, (g + 1) * group)
                    ],
                    axis=0,
                )
                part = tiles[s, :, g * group * width : (g + 1) * group * width]
                term = term + jnp.dot(part, khatri, preferred_element_type=F32)
            terms[s] = term

    cuts = [slots * k // 4 for k in range(5)]
    products(cuts[0], cuts[1])

    g_copy.wait_recv()
    strip_h[...] = gram_h[own_strip, :] + strip_core[...]
    gy_copies = [
        start(remote(strip_h, strip_y.at[d], gy_send.at[d], gy_recv.at[d], at_y(d)))
        for d in farthest_first(ny)
    ]
    products(cuts[1], cuts[2])

    for copy in gy_copies + gx_copies:
        copy.wait_recv()
    sum_h = strip_h[...]
    for d in range(1, ny):
        sum_h = sum_h + strip_y[d]
    sum_i = gram_i[own_strip, :]
    for d in range(1, ni):
        sum_i = sum_i + strip_x[d]
    strip[...] = sum_h * sum_i
    gram[own_strip, :] = strip[...]
    gz_copies = [
        start(remote(strip, gram.at[own_strip], gz_send.at[d], gz_recv.at[d], at_user(d)))
        for d in farthest_first(nu)
    ]
    products(cuts[2], cuts[4])

    chunks = width // share

    @pl.loop(0, user_blocks)
    def _(b):
        total = jnp.zeros((width, rank), F32)
        for s in range(slots):
            block = jnp.where(s < count[0], lax.rem(coords[s, 0], user_blocks), -1)
            hit = jnp.full((width, rank), block, jnp.int32) == b
            total = total + jnp.where(hit, terms[s], 0.0)
        for q in range(chunks):
            totals[q % 2, b * (chunks // 2) + q // 2] = total[q * share : (q + 1) * share]

    order = farthest_first(ni) + [0]

    def group_of(d):
        return pl.ds(((i + d) % ni) * ny, ny)

    rc_copies = {}
    for d in order:
        rc_copies[d] = start(
            remote(totals.at[1 - c, group_of(d)], from_core.at[group_of(d)], rc_send.at[d], rc_recv.at[d], sibling)
        )
    rx_copies = []
    for d in order:
        rc_copies[d].wait_recv()
        totals[c, group_of(d)] = totals[c, group_of(d)] + from_core[group_of(d)]
        if d:
            rx_copies.append(
                start(remote(totals.at[c, group_of(d)], from_x.at[d], rx_send.at[d], rx_recv.at[d], at_item(d)))
            )
    summed = totals[c, group_of(0)]
    for copy in rx_copies:
        copy.wait_recv()
    for d in range(1, ni):
        summed = summed + from_x[d]
    mine_x[...] = summed
    ry_copies = [
        start(remote(mine_x.at[(y + d) % ny], from_y.at[d], ry_send.at[d], ry_recv.at[d], at_y(d)))
        for d in farthest_first(ny)
    ]
    for copy in gz_copies:
        copy.wait_recv()
    gram_out[...] = gram[...]
    result = mine_x[y]
    for copy in ry_copies:
        copy.wait_recv()
    for d in range(1, ny):
        result = result + from_y[d]
    mttkrp_out[...] = result
    for copy in sent:
        copy.wait_send()


def sweep_kernel(mttkrp, gram, factor, out):
    share, rank = factor.shape
    lanes = 128
    pieces = rank // RANK_TILE
    weights = gram[...]
    current = factor[...]
    fitted = jnp.dot(current, weights, precision=lax.Precision.HIGHEST, preferred_element_type=F32)
    residual = mttkrp[...] - fitted

    def columns_first(x):
        return jnp.concatenate([x] * (lanes // share), axis=0).T

    rows = lax.broadcasted_iota(jnp.int32, (rank, rank), 0)
    cols = lax.broadcasted_iota(jnp.int32, (rank, rank), 1)
    pivot = jnp.sum(jnp.where(rows == cols, weights, 0.0), axis=1, keepdims=True)
    pivot = jnp.broadcast_to(pivot, (rank, lanes))
    scaled = weights / pivot
    start = columns_first(current)
    level = start + columns_first(residual) / pivot

    def split(x):
        return [x[g * RANK_TILE : (g + 1) * RANK_TILE] for g in range(pieces)]

    level, start, scaled = split(level), split(start), split(scaled)
    place = lax.broadcasted_iota(jnp.int32, (RANK_TILE, lanes), 0)
    fresh = []
    for g in range(pieces):
        done = jnp.zeros((RANK_TILE, lanes), F32)
        for k in range(RANK_TILE):
            r = g * RANK_TILE + k
            new = jnp.maximum(level[g], 0.0)
            change = (new - start[g])[k : k + 1, :]
            change = jnp.broadcast_to(change, (RANK_TILE, lanes))
            done = jnp.where(place == k, new, done)
            for h in range(g, pieces):
                weight = jnp.broadcast_to(scaled[h][:, r : r + 1], (RANK_TILE, lanes))
                level[h] = level[h] - weight * change
        fresh.append(done)
    out[...] = jnp.concatenate(fresh, axis=0).T[:share]


def per_device(nu, ni, nt, blocks, block_coords, block_count, a_factor, item_factor, hour_factor):
    tiles = blocks.reshape(blocks.shape[3:])
    coords = block_coords.reshape(block_coords.shape[3:])
    count = block_count.reshape((1,))
    slots, width, depth = tiles.shape
    share, rank = a_factor.shape
    ri, rh = item_factor.shape[0], hour_factor.shape[0]
    ny = nt // 2
    strip_rows = rank // nu
    vmem = pl.BlockSpec(memory_space=pltpu.VMEM)
    smem = pl.BlockSpec(memory_space=pltpu.SMEM)
    dma = pltpu.SemaphoreType.DMA
    mttkrp, gram = pl.pallas_call(
        functools.partial(exchange_kernel, nu, ni, nt),
        out_shape=(
            jax.ShapeDtypeStruct((share, rank), F32),
            jax.ShapeDtypeStruct((rank, rank), F32),
        ),
        in_specs=[smem, smem, pl.BlockSpec(memory_space=pltpu.MemorySpace.HBM), vmem, vmem],
        out_specs=(vmem, vmem),
        scratch_shapes=[
            pltpu.VMEM((nt, nu, ri, rank), BF16),
            pltpu.VMEM((ni, nu, rh, rank), BF16),
            pltpu.VMEM((slots, width, depth), BF16),
            pltpu.VMEM((slots, width, rank), F32),
            pltpu.VMEM((2, ni * ny, share, rank), F32),
            pltpu.VMEM((ni * ny, share, rank), F32),
            pltpu.VMEM((ni, ny, share, rank), F32),
            pltpu.VMEM((ny, share, rank), F32),
            pltpu.VMEM((ny, share, rank), F32),
            pltpu.VMEM((rank, rank), F32),
            pltpu.VMEM((rank, rank), F32),
            pltpu.VMEM((strip_rows, rank), F32),
            pltpu.VMEM((strip_rows, rank), F32),
            pltpu.VMEM((ny, strip_rows, rank), F32),
            pltpu.VMEM((ni, strip_rows, rank), F32),
            pltpu.VMEM((strip_rows, rank), F32),
            pltpu.VMEM((rank, rank), F32),
            dma((slots,)),
            dma((nu,)), dma((nu,)), dma((nu,)), dma((nu,)),
            dma((ny,)), dma((ny,)), dma((ny,)), dma((ny,)), dma((ni,)), dma((ni,)),
            dma, dma, dma((ny,)), dma((ny,)), dma((ni,)), dma((ni,)), dma((nu,)), dma((nu,)),
            dma((ni,)), dma((ni,)), dma((ni,)), dma((ni,)), dma((ny,)), dma((ny,)),
        ],
        compiler_params=pltpu.CompilerParams(
            collective_id=0, has_side_effects=True, vmem_limit_bytes=58 * 1024 * 1024
        ),
        name="exchange",
    )(coords, count, tiles, item_factor, hour_factor)
    return pl.pallas_call(
        sweep_kernel,
        out_shape=jax.ShapeDtypeStruct((share, rank), F32),
        in_specs=[vmem, vmem, vmem],
        out_specs=vmem,
        compiler_params=pltpu.CompilerParams(vmem_limit_bytes=8 * 1024 * 1024),
        name="sweep",
    )(mttkrp, gram, a_factor)


def solution(mesh):
    placed = (
        P("user", "item", "tm", None, None, None),
        P("user", "item", "tm", None, None),
        P("user", "item", "tm"),
        P(("user", "item", "tm"), None),
        P(("item", "user", "tm"), None),
        P(("tm", "user", "item"), None),
    )
    return jax.shard_map(
        functools.partial(per_device, mesh.shape["user"], mesh.shape["item"], mesh.shape["tm"]),
        mesh=mesh,
        in_specs=placed,
        out_specs=P(("user", "item", "tm"), None),
        check_vma=False,
    )
```

```python
import functools

import jax
import jax.numpy as jnp
from jax import lax
from jax.experimental import pallas as pl
from jax.experimental.pallas import tpu as pltpu
from jax.sharding import PartitionSpec as P

F32 = jnp.float32
BF16 = jnp.bfloat16
ROWS = 8
LANES = 128


def nearest_first(n):
    return sorted(range(1, n), key=lambda d: (min(d, n - d), d))


def farthest_first(n):
    return sorted(range(1, n), key=lambda d: (-min(d, n - d), d))


def self_product(rows):
    return lax.dot_general(rows, rows, (((0,), (0,)), ((), ())), preferred_element_type=F32)


def split(x, rows):
    return [x[k * rows : (k + 1) * rows] for k in range(x.shape[0] // rows)]


def columns_first(x):
    return jnp.concatenate([x] * (LANES // x.shape[0]), axis=0).T


def exchange_kernel(
    nu, ni, nt,
    coords_hbm, count_hbm, blocks, factor_hbm, item_hbm, hour_hbm,
    out,
    coords, count, factor, items, hours, tiles, terms, totals, from_core, from_x, mine_x, from_y,
    grams, g_core, g_mine, g_x, g_sum, g_y, gram,
    in_sem, tile_sem, z_send, z_recv, zh_send, zh_recv, y_send, y_recv, c_send, c_recv, x_send, x_recv,
    gc_send, gc_recv, gx_send, gx_recv, gy_send, gy_recv, gz_send, gz_recv,
    rc_send, rc_recv, rx_send, rx_recv, ry_send, ry_recv,
):
    ny = nt // 2
    u = lax.axis_index("user")
    i = lax.axis_index("item")
    t = lax.axis_index("tm")
    y, c = t // 2, t % 2
    slots, width, _ = tiles.shape
    ri, rh = item_hbm.shape[0], hour_hbm.shape[0]
    share, rank = factor.shape
    strip_rows = rank // nu

    def at_user(d):
        return {"user": (u + d) % nu}

    def at_item(d):
        return {"item": (i + d) % ni}

    def at_y(d):
        return {"tm": ((y + d) % ny) * 2 + c}

    sibling = {"tm": y * 2 + 1 - c}

    def remote(src, dst, send, recv, device):
        return pltpu.make_async_remote_copy(
            src_ref=src, dst_ref=dst, send_sem=send, recv_sem=recv,
            device_id=device, device_id_type=pl.DeviceIdType.MESH,
        )

    def tile_copy(s):
        return pltpu.make_async_copy(blocks.at[s], tiles.at[s], tile_sem.at[s])

    own_rows = [
        pltpu.make_async_copy(hour_hbm, hours.at[i, u], in_sem.at[0]),
        pltpu.make_async_copy(item_hbm, items.at[t, u], in_sem.at[1]),
    ]
    later = [
        pltpu.make_async_copy(factor_hbm, factor, in_sem.at[2]),
        pltpu.make_async_copy(coords_hbm, coords, in_sem.at[3]),
        pltpu.make_async_copy(count_hbm, count, in_sem.at[4]),
    ]
    for copy in own_rows:
        copy.start()

    barrier = pltpu.get_barrier_semaphore()
    partners = (
        [at_user(d) for d in farthest_first(nu)]
        + [at_item(d) for d in farthest_first(ni)]
        + [at_y(d) for d in farthest_first(ny)]
        + [sibling]
    )
    for device in partners:
        pl.semaphore_signal(barrier, inc=1, device_id=device, device_id_type=pl.DeviceIdType.MESH)
    for copy in own_rows:
        copy.wait()
    pl.semaphore_wait(barrier, len(partners))

    sent = []

    def start(copy):
        copy.start()
        sent.append(copy)
        return copy

    z_copies = []
    for d in farthest_first(nu):
        z_copies.append(start(remote(hours.at[i, u], hours.at[i, u], zh_send.at[d], zh_recv.at[d], at_user(d))))
        z_copies.append(start(remote(items.at[t, u], items.at[t, u], z_send.at[d], z_recv.at[d], at_user(d))))
    for copy in later:
        copy.start()
    for s in range(slots):
        tile_copy(s).start()
    for copy in z_copies:
        copy.wait_recv()

    y_copies = {}
    for d in farthest_first(ny):
        y_copies[d] = start(remote(items.at[t], items.at[t], y_send.at[d], y_recv.at[d], at_y(d)))
    x_copies = []
    for d in farthest_first(ni):
        x_copies.append(start(remote(hours.at[i], hours.at[i], x_send.at[d], x_recv.at[d], at_item(d))))
    c_copies = [start(remote(items.at[t], items.at[t], c_send.at[0], c_recv.at[0], sibling))]

    own_strip = pl.ds(pl.multiple_of(u * strip_rows, strip_rows), strip_rows)
    grams[0] = self_product(hours[i].reshape(nu * rh, rank))
    grams[1] = self_product(items[t].reshape(nu * ri, rank))
    gc_copy = start(remote(grams.at[:, own_strip], g_core, gc_send, gc_recv, sibling))
    gc_copy.wait_recv()
    g_mine[...] = grams[:, own_strip] + g_core[...]
    gx_copies = [
        start(remote(g_mine, g_x.at[d], gx_send.at[d], gx_recv.at[d], at_item(d)))
        for d in farthest_first(ni)
    ]

    for d in nearest_first(ny):
        y_copies[d].wait_recv()
        source = ((y + ny - d) % ny) * 2 + c
        c_copies.append(
            start(remote(items.at[source], items.at[source], c_send.at[d], c_recv.at[d], sibling))
        )
    for copy in gx_copies:
        copy.wait_recv()
    g_total = g_mine[...]
    for d in range(1, ni):
        g_total = g_total + g_x[d]
    g_sum[...] = g_total
    gy_copies = [
        start(remote(g_sum, g_y.at[d], gy_send.at[d], gy_recv.at[d], at_y(d)))
        for d in farthest_first(ny)
    ]
    for copy in later:
        copy.wait()
    for copy in x_copies:
        copy.wait_recv()
    for copy in c_copies:
        copy.wait_recv()

    user_blocks = (share * ni * nt) // width
    item_blocks = (ri * nu * nt) // width
    hour_blocks = (rh * nu * ni) // width
    span = width // ri
    per_user = nt // span
    group = 16

    @pl.loop(0, slots)
    def _(s):
        tile_copy(s).wait()
        item_block = lax.rem(coords[1, 0, s], item_blocks)
        hour_block = lax.rem(coords[2, 0, s], hour_blocks)
        item_rows = (
            items[pl.ds(lax.rem(item_block, per_user) * span, span), lax.div(item_block, per_user)]
            .astype(F32)
            .reshape(width, rank)
        )
        hour_rows = hours[:, hour_block].astype(F32).reshape(width, rank)
        term = jnp.zeros((width, rank), F32)
        for g in range(width // group):
            khatri = jnp.concatenate(
                [(item_rows[j : j + 1, :] * hour_rows).astype(BF16) for j in range(g * group, (g + 1) * group)],
                axis=0,
            )
            part = tiles[s, :, g * group * width : (g + 1) * group * width]
            term = term + jnp.dot(part, khatri, preferred_element_type=F32)
        terms[s] = term

    chunks = width // share

    @pl.loop(0, user_blocks)
    def _(b):
        total = jnp.zeros((width, rank), F32)
        for s in range(slots):
            block = jnp.where(s < count[0, 0, 0], lax.rem(coords[0, 0, s], user_blocks), -1)
            hit = jnp.full((width, rank), block, jnp.int32) == b
            total = total + jnp.where(hit, terms[s], 0.0)
        for q in range(chunks):
            totals[q % 2, b * (chunks // 2) + q // 2] = total[q * share : (q + 1) * share]

    order = farthest_first(ni) + [0]

    def group_of(d):
        return pl.ds(((i + d) % ni) * ny, ny)

    rc_copies = {}
    for d in order:
        rc_copies[d] = start(
            remote(totals.at[1 - c, group_of(d)], from_core.at[group_of(d)], rc_send.at[d], rc_recv.at[d], sibling)
        )
    rx_copies = []
    for d in order:
        rc_copies[d].wait_recv()
        totals[c, group_of(d)] = totals[c, group_of(d)] + from_core[group_of(d)]
        if d:
            rx_copies.append(
                start(remote(totals.at[c, group_of(d)], from_x.at[d], rx_send.at[d], rx_recv.at[d], at_item(d)))
            )

    for copy in gy_copies:
        copy.wait_recv()
    g_total = g_sum[...]
    for d in range(1, ny):
        g_total = g_total + g_y[d]
    gram[own_strip, :] = g_total[0] * g_total[1]
    gz_copies = [
        start(remote(gram.at[own_strip], gram.at[own_strip], gz_send.at[d], gz_recv.at[d], at_user(d)))
        for d in farthest_first(nu)
    ]

    summed = totals[c, group_of(0)]
    for copy in rx_copies:
        copy.wait_recv()
    for d in range(1, ni):
        summed = summed + from_x[d]
    mine_x[...] = summed
    ry_copies = [
        start(remote(mine_x.at[(y + d) % ny], from_y.at[d], ry_send.at[d], ry_recv.at[d], at_y(d)))
        for d in farthest_first(ny)
    ]

    for copy in gz_copies:
        copy.wait_recv()
    weights = gram[...]
    current = factor[...]
    fitted = jnp.dot(current, weights, precision=lax.Precision.HIGHEST, preferred_element_type=F32)
    rows = lax.broadcasted_iota(jnp.int32, (rank, rank), 0)
    cols = lax.broadcasted_iota(jnp.int32, (rank, rank), 1)
    pivot = jnp.sum(jnp.where(rows == cols, weights, 0.0), axis=1, keepdims=True)
    pivot = jnp.broadcast_to(pivot, (rank, LANES))
    scaled = weights / pivot
    before = columns_first(current)

    for copy in ry_copies:
        copy.wait_recv()
    mttkrp = mine_x[y]
    for d in range(1, ny):
        mttkrp = mttkrp + from_y[d]

    level = before + columns_first(mttkrp - fitted) / pivot
    place = lax.broadcasted_iota(jnp.int32, (ROWS, LANES), 0)
    fresh = []
    for g in range(rank // ROWS):
        low, high = g * ROWS, (g + 1) * ROWS
        head, rest = level[:ROWS], level[ROWS:]
        old = before[low:high]
        done = head
        for k in range(ROWS):
            new = jnp.maximum(head, 0.0)
            change = jnp.broadcast_to((new - old)[k : k + 1], (ROWS, LANES))
            done = jnp.where(place == k, new, done)
            if k < ROWS - 1:
                head = head - jnp.broadcast_to(scaled[low:high, low + k : low + k + 1], (ROWS, LANES)) * change
            if rest.shape[0]:
                full = jnp.concatenate([change] * (rest.shape[0] // ROWS), axis=0)
                rest = rest - jnp.broadcast_to(scaled[high:, low + k : low + k + 1], rest.shape) * full
        fresh.append(done)
        level = rest
    out[...] = jnp.concatenate(fresh, axis=0).T[:share]
    for copy in sent:
        copy.wait_send()


def per_device(nu, ni, nt, blocks, block_coords, block_count, a_factor, item_factor, hour_factor):
    tiles = blocks.reshape(blocks.shape[3:])
    slots, width, depth = tiles.shape
    coords = jnp.transpose(block_coords, (0, 1, 4, 2, 3)).reshape(3, 1, slots)
    count = block_count.reshape((1, 1, 1))
    share, rank = a_factor.shape
    ri, rh = item_factor.shape[0], hour_factor.shape[0]
    ny = nt // 2
    strip_rows = rank // nu
    hbm = pl.BlockSpec(memory_space=pltpu.MemorySpace.HBM)
    vmem, smem, dma = pltpu.VMEM, pltpu.SMEM, pltpu.SemaphoreType.DMA
    return pl.pallas_call(
        functools.partial(exchange_kernel, nu, ni, nt),
        out_shape=jax.ShapeDtypeStruct((share, rank), F32),
        in_specs=[hbm] * 6,
        out_specs=pl.BlockSpec(memory_space=pltpu.VMEM),
        scratch_shapes=[
            smem((3, 1, slots), jnp.int32),
            smem((1, 1, 1), jnp.int32),
            vmem((share, rank), F32),
            vmem((nt, nu, ri, rank), BF16),
            vmem((ni, nu, rh, rank), BF16),
            vmem((slots, width, depth), BF16),
            vmem((slots, width, rank), F32),
            vmem((2, ni * ny, share, rank), F32),
            vmem((ni * ny, share, rank), F32),
            vmem((ni, ny, share, rank), F32),
            vmem((ny, share, rank), F32),
            vmem((ny, share, rank), F32),
            vmem((2, rank, rank), F32),
            vmem((2, strip_rows, rank), F32),
            vmem((2, strip_rows, rank), F32),
            vmem((ni, 2, strip_rows, rank), F32),
            vmem((2, strip_rows, rank), F32),
            vmem((ny, 2, strip_rows, rank), F32),
            vmem((rank, rank), F32),
            dma((5,)),
            dma((slots,)),
            dma((nu,)), dma((nu,)), dma((nu,)), dma((nu,)),
            dma((ny,)), dma((ny,)), dma((ny,)), dma((ny,)), dma((ni,)), dma((ni,)),
            dma, dma, dma((ni,)), dma((ni,)), dma((ny,)), dma((ny,)), dma((nu,)), dma((nu,)),
            dma((ni,)), dma((ni,)), dma((ni,)), dma((ni,)), dma((ny,)), dma((ny,)),
        ],
        compiler_params=pltpu.CompilerParams(
            collective_id=0, has_side_effects=True, vmem_limit_bytes=58 * 1024 * 1024
        ),
        name="exchange",
    )(coords, count, tiles, a_factor, item_factor, hour_factor)


def solution(mesh):
    placed = (
        P("user", "item", "tm", None, None, None),
        P("user", "item", "tm", None, None),
        P("user", "item", "tm"),
        P(("user", "item", "tm"), None),
        P(("item", "user", "tm"), None),
        P(("tm", "user", "item"), None),
    )
    return jax.shard_map(
        functools.partial(per_device, mesh.shape["user"], mesh.shape["item"], mesh.shape["tm"]),
        mesh=mesh,
        in_specs=placed,
        out_specs=P(("user", "item", "tm"), None),
        check_vma=False,
    )
```

```python
import functools

import jax
import jax.numpy as jnp
from jax import lax
from jax.experimental import pallas as pl
from jax.experimental.pallas import tpu as pltpu
from jax.sharding import PartitionSpec as P

F32 = jnp.float32
BF16 = jnp.bfloat16
ROWS = 8
LANES = 128


def nearest_first(n):
    return sorted(range(1, n), key=lambda d: (min(d, n - d), d))


def farthest_first(n):
    return sorted(range(1, n), key=lambda d: (-min(d, n - d), d))


def self_product(rows):
    return lax.dot_general(rows, rows, (((0,), (0,)), ((), ())), preferred_element_type=F32)


def split(x, rows):
    return [x[k * rows : (k + 1) * rows] for k in range(x.shape[0] // rows)]


def columns_first(x):
    return jnp.concatenate([x] * (LANES // x.shape[0]), axis=0).T


def exchange_kernel(
    nu, ni, nt,
    coords_hbm, count_hbm, blocks, factor_hbm, item_hbm, hour_hbm,
    before_out, scaled_out, level_out,
    coords, count, factor, items, hours, tiles, terms, totals, from_core, from_x, mine_x, from_y,
    grams, g_core, g_y, g_sum, g_x, g_mine, g_other, gram,
    in_sem, tile_sem, z_send, z_recv, zh_send, zh_recv, y_send, y_recv, c_send, c_recv, x_send, x_recv,
    gc_send, gc_recv, gx_send, gx_recv, gy_send, gy_recv, go_send, go_recv, ga_send, ga_recv,
    rc_send, rc_recv, rx_send, rx_recv, ry_send, ry_recv,
):
    ny = nt // 2
    u = lax.axis_index("user")
    i = lax.axis_index("item")
    t = lax.axis_index("tm")
    y, c = t // 2, t % 2
    slots, width, _ = tiles.shape
    ri, rh = item_hbm.shape[0], hour_hbm.shape[0]
    share, rank = factor.shape
    strip_rows = rank // ny

    def at_user(d):
        return {"user": (u + d) % nu}

    def at_item(d):
        return {"item": (i + d) % ni}

    def at_y(d):
        return {"tm": ((y + d) % ny) * 2 + c}

    sibling = {"tm": y * 2 + 1 - c}

    def remote(src, dst, send, recv, device):
        return pltpu.make_async_remote_copy(
            src_ref=src, dst_ref=dst, send_sem=send, recv_sem=recv,
            device_id=device, device_id_type=pl.DeviceIdType.MESH,
        )

    def tile_copy(s):
        return pltpu.make_async_copy(blocks.at[s], tiles.at[s], tile_sem.at[s])

    own_rows = [
        pltpu.make_async_copy(item_hbm, items.at[t, u], z_recv.at[u]),
        pltpu.make_async_copy(hour_hbm, hours.at[i, u], zh_recv.at[u]),
    ]
    later = [
        pltpu.make_async_copy(factor_hbm, factor, in_sem.at[0]),
        pltpu.make_async_copy(coords_hbm, coords, in_sem.at[1]),
        pltpu.make_async_copy(count_hbm, count, in_sem.at[2]),
    ]

    barrier = pltpu.get_barrier_semaphore()
    partners = (
        [at_user(d) for d in farthest_first(nu)]
        + [at_item(d) for d in farthest_first(ni)]
        + [at_y(d) for d in farthest_first(ny)]
        + [sibling]
    )
    for device in partners:
        pl.semaphore_signal(barrier, inc=1, device_id=device, device_id_type=pl.DeviceIdType.MESH)
    for copy in own_rows:
        copy.start()
    pl.semaphore_wait(barrier, len(partners))

    sent = []

    def start(copy):
        copy.start()
        sent.append(copy)
        return copy

    for d in farthest_first(nu):
        start(remote(item_hbm, items.at[t, u], z_send.at[d], z_recv.at[u], at_user(d)))
    for d in farthest_first(nu):
        start(remote(hour_hbm, hours.at[i, u], zh_send.at[d], zh_recv.at[u], at_user(d)))
    for copy in later:
        copy.start()
    for s in range(slots):
        tile_copy(s).start()

    def wait_rows(rows, ref, send, recv):
        for v in range(nu)[rows]:
            remote(ref.at[v], ref.at[v], send.at[0], recv.at[v], at_user(1)).wait_recv()

    halves = [slice(0, nu // 2), slice(nu // 2, nu)]
    y_copies, c_copies = [{}, {}], []
    for k, half in enumerate(halves):
        wait_rows(half, items.at[t], z_send, z_recv)
        part = items.at[t, half]
        for d in farthest_first(ny):
            y_copies[k][d] = start(remote(part, part, y_send.at[k, d], y_recv.at[k, d], at_y(d)))
        c_copies.append(start(remote(part, part, c_send.at[k, 0], c_recv.at[k, 0], sibling)))
    wait_rows(slice(0, nu), hours.at[i], zh_send, zh_recv)
    x_copies = []
    for d in farthest_first(ni):
        x_copies.append(start(remote(hours.at[i], hours.at[i], x_send.at[d], x_recv.at[d], at_item(d))))

    def strip(v):
        return pl.ds(pl.multiple_of(v * strip_rows, strip_rows), strip_rows)

    grams[0] = self_product(hours[i].reshape(nu * rh, rank))
    grams[1] = self_product(items[t].reshape(nu * ri, rank))
    gc_copy = start(remote(grams.at[1 - c], g_core, gc_send, gc_recv, sibling))
    gc_copy.wait_recv()
    grams[c] = grams[c] + g_core[...]
    gy_copies = [
        start(remote(grams.at[c, strip((y + d) % ny)], g_y.at[d], gy_send.at[d], gy_recv.at[d], at_y(d)))
        for d in farthest_first(ny)
    ]

    for k, half in enumerate(halves):
        for d in nearest_first(ny):
            y_copies[k][d].wait_recv()
            part = items.at[((y + ny - d) % ny) * 2 + c, half]
            c_copies.append(start(remote(part, part, c_send.at[k, d], c_recv.at[k, d], sibling)))
    for copy in later:
        copy.wait()
    for copy in x_copies:
        copy.wait_recv()
    for copy in c_copies:
        copy.wait_recv()

    user_blocks = (share * ni * nt) // width
    item_blocks = (ri * nu * nt) // width
    hour_blocks = (rh * nu * ni) // width
    span = width // ri
    per_user = nt // span
    group = 16

    def product(s):
        tile_copy(s).wait()
        item_block = lax.rem(coords[1, 0, s], item_blocks)
        hour_block = lax.rem(coords[2, 0, s], hour_blocks)
        item_rows = (
            items[pl.ds(lax.rem(item_block, per_user) * span, span), lax.div(item_block, per_user)]
            .astype(F32)
            .reshape(width, rank)
        )
        hour_rows = hours[:, hour_block].astype(F32).reshape(width, rank)
        term = jnp.zeros((width, rank), F32)
        for g in range(width // group):
            khatri = jnp.concatenate(
                [(item_rows[j : j + 1, :] * hour_rows).astype(BF16) for j in range(g * group, (g + 1) * group)],
                axis=0,
            )
            part = tiles[s, :, g * group * width : (g + 1) * group * width]
            term = term + jnp.dot(part, khatri, preferred_element_type=F32)
        terms[s] = term

    pl.loop(0, slots // 2)(product)
    for copy in gy_copies:
        copy.wait_recv()
    g_total = grams[c, strip(y)]
    for d in range(1, ny):
        g_total = g_total + g_y[d]
    g_sum[...] = g_total
    gx_copies = [
        start(remote(g_sum, g_x.at[d], gx_send.at[d], gx_recv.at[d], at_item(d)))
        for d in farthest_first(ni)
    ]
    pl.loop(slots // 2, slots)(product)

    chunks = width // share
    reach = ny // 4
    near = 2 * reach + 1

    @pl.loop(0, user_blocks)
    def _(b):
        total = jnp.zeros((width, rank), F32)
        for s in range(slots):
            block = jnp.where(s < count[0, 0, 0], lax.rem(coords[0, 0, s], user_blocks), -1)
            hit = jnp.full((width, rank), block, jnp.int32) == b
            total = total + jnp.where(hit, terms[s], 0.0)
        for q in range(chunks):
            chip = b * (chunks // 2) + q // 2
            place = (chip % ny + ny - y + reach) % ny
            totals[q % 2, chip // ny, place] = total[q * share : (q + 1) * share]

    parts = [pl.ds(near, ny - near), pl.ds(0, near)]
    rc_copies = [
        start(
            remote(
                totals.at[1 - c, :, part], from_core.at[:, part], rc_send.at[k], rc_recv.at[k], sibling
            )
        )
        for k, part in enumerate(parts)
    ]
    rx_copies = [[], []]
    for k, part in enumerate(parts):
        rc_copies[k].wait_recv()
        totals[c, :, part] = totals[c, :, part] + from_core[:, part]
        for d in farthest_first(ni):
            rx_copies[k].append(
                start(
                    remote(
                        totals.at[c, (i + d) % ni, part], from_x.at[d, part],
                        rx_send.at[k, d], rx_recv.at[k, d], at_item(d),
                    )
                )
            )
    for copy in gx_copies:
        copy.wait_recv()
    g_total = g_sum[...]
    for d in range(1, ni):
        g_total = g_total + g_x[d]
    g_mine[...] = g_total
    go_copy = start(remote(g_mine, g_other, go_send, go_recv, sibling))
    go_copy.wait_recv()
    gram[strip(y), :] = g_mine[...] * g_other[...]
    ga_copies = [
        start(remote(gram.at[strip(y)], gram.at[strip(y)], ga_send.at[d], ga_recv.at[d], at_y(d)))
        for d in farthest_first(ny)
    ]

    ry_copies = []
    for k, part in enumerate(parts):
        for copy in rx_copies[k]:
            copy.wait_recv()
        summed = totals[c, i, part]
        for d in range(1, ni):
            summed = summed + from_x[d, part]
        mine_x[part] = summed
        for d in farthest_first(ny):
            place = (d + reach) % ny
            if (place >= near) == (k == 0):
                ry_copies.append(
                    start(remote(mine_x.at[place], from_y.at[d], ry_send.at[d], ry_recv.at[d], at_y(d)))
                )

    for copy in ga_copies:
        copy.wait_recv()
    weights = gram[...]
    current = factor[...]
    fitted = jnp.dot(current, weights, precision=lax.Precision.HIGHEST, preferred_element_type=F32)
    rows = lax.broadcasted_iota(jnp.int32, (rank, rank), 0)
    cols = lax.broadcasted_iota(jnp.int32, (rank, rank), 1)
    pivot = jnp.sum(jnp.where(rows == cols, weights, 0.0), axis=1, keepdims=True)
    pivot = jnp.broadcast_to(pivot, (rank, LANES))
    scaled = weights / pivot
    before = columns_first(current)

    for copy in ry_copies:
        copy.wait_recv()
    mttkrp = mine_x[reach]
    for d in range(1, ny):
        mttkrp = mttkrp + from_y[d]

    before_out[...] = before
    scaled_out[...] = scaled
    level_out[...] = before + columns_first(mttkrp - fitted) / pivot
    for copy in sent:
        copy.wait_send()


def sweep_kernel(before_ref, scaled_ref, level_ref, out):
    rank, share = level_ref.shape[0], out.shape[0]
    before, scaled, level = before_ref[...], scaled_ref[...], level_ref[...]
    place = lax.broadcasted_iota(jnp.int32, (ROWS, LANES), 0)
    fresh = []
    for g in range(rank // ROWS):
        low, high = g * ROWS, (g + 1) * ROWS
        head, rest = level[:ROWS], level[ROWS:]
        old = before[low:high]
        done = head
        for k in range(ROWS):
            new = jnp.maximum(head, 0.0)
            change = jnp.broadcast_to((new - old)[k : k + 1], (ROWS, LANES))
            done = jnp.where(place == k, new, done)
            if k < ROWS - 1:
                head = head - jnp.broadcast_to(scaled[low:high, low + k : low + k + 1], (ROWS, LANES)) * change
            if rest.shape[0]:
                full = jnp.concatenate([change] * (rest.shape[0] // ROWS), axis=0)
                rest = rest - jnp.broadcast_to(scaled[high:, low + k : low + k + 1], rest.shape) * full
        fresh.append(done)
        level = rest
    out[...] = jnp.concatenate(fresh, axis=0).T[:share]


def per_device(nu, ni, nt, blocks, block_coords, block_count, a_factor, item_factor, hour_factor):
    tiles = blocks.reshape(blocks.shape[3:])
    slots, width, depth = tiles.shape
    coords = jnp.transpose(block_coords, (0, 1, 4, 2, 3)).reshape(3, 1, slots)
    count = block_count.reshape((1, 1, 1))
    share, rank = a_factor.shape
    ri, rh = item_factor.shape[0], hour_factor.shape[0]
    ny = nt // 2
    strip_rows = rank // ny
    hbm = pl.BlockSpec(memory_space=pltpu.MemorySpace.HBM)
    on_chip = pl.BlockSpec(memory_space=pltpu.VMEM)
    vmem, smem, dma = pltpu.VMEM, pltpu.SMEM, pltpu.SemaphoreType.DMA
    ready = pl.pallas_call(
        functools.partial(exchange_kernel, nu, ni, nt),
        out_shape=(vmem((rank, LANES), F32), vmem((rank, rank), F32), vmem((rank, LANES), F32)),
        in_specs=[hbm] * 6,
        out_specs=[on_chip] * 3,
        scratch_shapes=[
            smem((3, 1, slots), jnp.int32),
            smem((1, 1, 1), jnp.int32),
            vmem((share, rank), F32),
            vmem((nt, nu, ri, rank), BF16),
            vmem((ni, nu, rh, rank), BF16),
            vmem((slots, width, depth), BF16),
            vmem((slots, width, rank), F32),
            vmem((2, ni, ny, share, rank), F32),
            vmem((ni, ny, share, rank), F32),
            vmem((ni, ny, share, rank), F32),
            vmem((ny, share, rank), F32),
            vmem((ny, share, rank), F32),
            vmem((2, rank, rank), F32),
            vmem((rank, rank), F32),
            vmem((ny, strip_rows, rank), F32),
            vmem((strip_rows, rank), F32),
            vmem((ni, strip_rows, rank), F32),
            vmem((strip_rows, rank), F32),
            vmem((strip_rows, rank), F32),
            vmem((rank, rank), F32),
            dma((3,)),
            dma((slots,)),
            dma((nu,)), dma((nu,)), dma((nu,)), dma((nu,)),
            dma((2, ny)), dma((2, ny)), dma((2, ny)), dma((2, ny)), dma((ni,)), dma((ni,)),
            dma, dma, dma((ni,)), dma((ni,)), dma((ny,)), dma((ny,)), dma, dma, dma((ny,)), dma((ny,)),
            dma((2,)), dma((2,)), dma((2, ni)), dma((2, ni)), dma((ny,)), dma((ny,)),
        ],
        compiler_params=pltpu.CompilerParams(
            collective_id=0, has_side_effects=True, vmem_limit_bytes=58 * 1024 * 1024
        ),
        name="exchange",
    )(coords, count, tiles, a_factor, item_factor, hour_factor)
    return pl.pallas_call(
        sweep_kernel,
        out_shape=jax.ShapeDtypeStruct((share, rank), F32),
        in_specs=[on_chip] * 3,
        out_specs=on_chip,
        compiler_params=pltpu.CompilerParams(vmem_limit_bytes=8 * 1024 * 1024),
        name="sweep",
    )(*ready)


def solution(mesh):
    placed = (
        P("user", "item", "tm", None, None, None),
        P("user", "item", "tm", None, None),
        P("user", "item", "tm"),
        P(("user", "item", "tm"), None),
        P(("item", "user", "tm"), None),
        P(("tm", "user", "item"), None),
    )
    return jax.shard_map(
        functools.partial(per_device, mesh.shape["user"], mesh.shape["item"], mesh.shape["tm"]),
        mesh=mesh,
        in_specs=placed,
        out_specs=P(("user", "item", "tm"), None),
        check_vma=False,
    )
```

```python
import functools

import jax
import jax.numpy as jnp
from jax import lax
from jax.experimental import pallas as pl
from jax.experimental.pallas import tpu as pltpu
from jax.sharding import PartitionSpec as P

F32 = jnp.float32
BF16 = jnp.bfloat16
ROWS = 8
LANES = 128


def nearest_first(n):
    return sorted(range(1, n), key=lambda d: (min(d, n - d), d))


def farthest_first(n):
    return sorted(range(1, n), key=lambda d: (-min(d, n - d), d))


def self_product(rows):
    return lax.dot_general(rows, rows, (((0,), (0,)), ((), ())), preferred_element_type=F32)


def split(x, rows):
    return [x[k * rows : (k + 1) * rows] for k in range(x.shape[0] // rows)]


def column_places(rank):
    places, start = [], 0
    for r in range(rank):
        first_row = r // ROWS * ROWS
        places.append((first_row, start))
        start += rank - first_row
    return places


def columns_first(x):
    return jnp.concatenate([x] * (LANES // x.shape[0]), axis=0).T


def exchange_kernel(
    nu, ni, nt,
    coords_hbm, count_hbm, blocks, factor_hbm, item_hbm, hour_hbm,
    wide_out, level_out,
    coords, count, factor, rows_u, items, hours, tiles, terms, totals, from_core, from_x, mine_x, from_y,
    grams, g_core, g_y, g_sum, g_x, g_mine, g_other, gram,
    in_sem, tile_sem, z_send, z_recv, y_send, y_recv, c_send, c_recv, x_send, x_recv,
    gc_send, gc_recv, gx_send, gx_recv, gy_send, gy_recv, go_send, go_recv, ga_send, ga_recv,
    rc_send, rc_recv, rx_send, rx_recv, ry_send, ry_recv,
):
    ny = nt // 2
    u = lax.axis_index("user")
    i = lax.axis_index("item")
    t = lax.axis_index("tm")
    y, c = t // 2, t % 2
    slots, width, _ = tiles.shape
    ri, rh = item_hbm.shape[0], hour_hbm.shape[0]
    share, rank = factor.shape
    strip_rows = rank // ny
    pieces = rh // ri
    reach = ny // 4
    near = 2 * reach + 1

    def at_user(d):
        return {"user": (u + d) % nu}

    def at_item(d):
        return {"item": (i + d) % ni}

    def at_y(d):
        return {"tm": ((y + d) % ny) * 2 + c}

    def at_other(d):
        return {"tm": ((y + d) % ny) * 2 + 1 - c}

    sibling = at_other(0)

    def remote(src, dst, send, recv, device):
        return pltpu.make_async_remote_copy(
            src_ref=src, dst_ref=dst, send_sem=send, recv_sem=recv,
            device_id=device, device_id_type=pl.DeviceIdType.MESH,
        )

    def tile_copy(s):
        return pltpu.make_async_copy(blocks.at[s], tiles.at[s], tile_sem.at[s])

    own_rows = [pltpu.make_async_copy(item_hbm, rows_u.at[u, 0], in_sem.at[3])] + [
        pltpu.make_async_copy(hour_hbm.at[q * ri : (q + 1) * ri], rows_u.at[u, 1 + q], in_sem.at[4 + q])
        for q in range(pieces)
    ]
    later = [
        pltpu.make_async_copy(factor_hbm, factor, in_sem.at[0]),
        pltpu.make_async_copy(coords_hbm, coords, in_sem.at[1]),
        pltpu.make_async_copy(count_hbm, count, in_sem.at[2]),
    ]

    for copy in own_rows:
        copy.start()

    barrier = pltpu.get_barrier_semaphore()
    partners = (
        [at_user(d) for d in farthest_first(nu)]
        + [at_item(d) for d in farthest_first(ni)]
        + [at_y(d) for d in farthest_first(ny)]
        + [sibling]
    )
    for device in partners:
        pl.semaphore_signal(barrier, inc=1, device_id=device, device_id_type=pl.DeviceIdType.MESH)
    pl.semaphore_wait(barrier, len(partners))

    for copy in own_rows:
        copy.wait()
    sent = []

    def start(copy):
        copy.start()
        sent.append(copy)
        return copy

    for d in farthest_first(nu):
        start(remote(rows_u.at[u], rows_u.at[u], z_send.at[d], z_recv.at[u], at_user(d)))
    for copy in later:
        copy.start()
    for s in range(slots):
        tile_copy(s).start()
    for v in range(nu):
        pl.when(u != v)(remote(rows_u.at[v], rows_u.at[v], z_send.at[0], z_recv.at[v], at_user(1)).wait_recv)

    own_items, own_hours = rows_u.at[:, 0], rows_u.at[:, pl.ds(1, pieces)]
    y_copies = {
        d: start(remote(own_items, items.at[c, (reach + ny - d) % ny], y_send.at[d], y_recv.at[d], at_y(d)))
        for d in farthest_first(ny)
    }
    x_copies = [
        start(remote(own_hours, hours.at[i], x_send.at[d], x_recv.at[d], at_item(d))) for d in farthest_first(ni)
    ]
    items[c, reach] = own_items[...]
    hours[i] = own_hours[...]

    def strip(v):
        return pl.ds(pl.multiple_of(v * strip_rows, strip_rows), strip_rows)

    grams[0] = self_product(own_hours[...].reshape(nu * rh, rank))
    grams[1] = self_product(own_items[...].reshape(nu * ri, rank))
    gc_copy = start(remote(grams.at[1 - c], g_core, gc_send, gc_recv, sibling))
    gc_copy.wait_recv()
    grams[c] = grams[c] + g_core[...]
    gy_copies = [
        start(remote(grams.at[c, strip((y + d) % ny)], g_y.at[d], gy_send.at[d], gy_recv.at[d], at_y(d)))
        for d in farthest_first(ny)
    ]

    c_copies = []
    for k, part in enumerate([pl.ds(0, near), pl.ds(near, ny - near)]):
        for d in nearest_first(ny):
            if ((reach + ny - d) % ny >= near) == bool(k):
                y_copies[d].wait_recv()
        c_copies.append(start(remote(items.at[c, part], items.at[c, part], c_send.at[k], c_recv.at[k], sibling)))
    for copy in later:
        copy.wait()
    for copy in x_copies:
        copy.wait_recv()
    for copy in c_copies:
        copy.wait_recv()

    user_blocks = (share * ni * nt) // width
    item_blocks = (ri * nu * nt) // width
    hour_blocks = (rh * nu * ni) // width
    span = width // ri
    per_user = nt // span
    group = 16

    def product(s):
        tile_copy(s).wait()
        item_block = lax.rem(coords[1, 0, s], item_blocks)
        hour_block = lax.rem(coords[2, 0, s], hour_blocks)
        chip = lax.div(lax.rem(item_block, per_user) * span, 2) + ny - y + reach
        owner = lax.div(item_block, per_user)
        item_rows = [
            items[core, lax.rem(chip + step, ny), owner] for step in range(span // 2) for core in range(2)
        ]
        item_rows = jnp.concatenate([rows.astype(F32) for rows in item_rows], axis=0)
        hour_rows = hours[:, hour_block].astype(F32).reshape(width, rank)
        term = jnp.zeros((width, rank), F32)
        for g in range(width // group):
            khatri = jnp.concatenate(
                [(item_rows[j : j + 1, :] * hour_rows).astype(BF16) for j in range(g * group, (g + 1) * group)],
                axis=0,
            )
            part = tiles[s, :, g * group * width : (g + 1) * group * width]
            term = term + jnp.dot(part, khatri, preferred_element_type=F32)
        terms[s] = term

    pl.loop(0, slots // 2)(product)
    for copy in gy_copies:
        copy.wait_recv()
    g_total = grams[c, strip(y)]
    for d in range(1, ny):
        g_total = g_total + g_y[d]
    g_sum[...] = g_total
    gx_copies = [
        start(remote(g_sum, g_x.at[d], gx_send.at[d], gx_recv.at[d], at_item(d)))
        for d in farthest_first(ni)
    ]
    pl.loop(slots // 2, slots)(product)

    chunks = width // share

    @pl.loop(0, user_blocks)
    def _(b):
        total = jnp.zeros((width, rank), F32)
        for s in range(slots):
            block = jnp.where(s < count[0, 0, 0], lax.rem(coords[0, 0, s], user_blocks), -1)
            hit = jnp.full((width, rank), block, jnp.int32) == b
            total = total + jnp.where(hit, terms[s], 0.0)
        for q in range(chunks):
            chip = b * (chunks // 2) + q // 2
            place = (chip % ny + ny - y + reach) % ny
            totals[q % 2, chip // ny, place] = total[q * share : (q + 1) * share]

    parts = [pl.ds(near, ny - near), pl.ds(0, near)]
    rc_copies = [
        start(
            remote(
                totals.at[1 - c, :, part], from_core.at[:, part], rc_send.at[k], rc_recv.at[k], sibling
            )
        )
        for k, part in enumerate(parts)
    ]
    rx_copies = [[], []]
    for k, part in enumerate(parts):
        rc_copies[k].wait_recv()
        totals[c, :, part] = totals[c, :, part] + from_core[:, part]
        for d in farthest_first(ni):
            rx_copies[k].append(
                start(
                    remote(
                        totals.at[c, (i + d) % ni, part], from_x.at[d, part],
                        rx_send.at[k, d], rx_recv.at[k, d], at_item(d),
                    )
                )
            )
    for copy in gx_copies:
        copy.wait_recv()
    g_total = g_sum[...]
    for d in range(1, ni):
        g_total = g_total + g_x[d]
    g_mine[...] = g_total
    go_copy = start(remote(g_mine, g_other, go_send, go_recv, sibling))
    go_copy.wait_recv()
    gram[strip(y), :] = g_mine[...] * g_other[...]
    ga_copies = [
        start(remote(gram.at[strip(y)], gram.at[strip(y)], ga_send.at[d], ga_recv.at[d], at_y(d)))
        for d in farthest_first(ny)
    ]

    ry_copies = []
    for k, part in enumerate(parts):
        for copy in rx_copies[k]:
            copy.wait_recv()
        summed = totals[c, i, part]
        for d in range(1, ni):
            summed = summed + from_x[d, part]
        mine_x[part] = summed
        for d in farthest_first(ny):
            place = (d + reach) % ny
            if (place >= near) == (k == 0):
                ry_copies.append(
                    start(remote(mine_x.at[place], from_y.at[d], ry_send.at[d], ry_recv.at[d], at_y(d)))
                )

    for copy in ga_copies:
        copy.wait_recv()
    weights = gram[...]
    current = factor[...]
    rows = lax.broadcasted_iota(jnp.int32, (rank, rank), 0)
    cols = lax.broadcasted_iota(jnp.int32, (rank, rank), 1)
    fitted = jnp.dot(
        current, jnp.where(rows > cols, weights, 0.0), precision=lax.Precision.HIGHEST, preferred_element_type=F32
    )
    pivot = jnp.sum(jnp.where(rows == cols, weights, 0.0), axis=1, keepdims=True)
    pivot = jnp.broadcast_to(pivot, (rank, LANES))
    scaled = weights / pivot
    for r, (first_row, start_row) in enumerate(column_places(rank)):
        rows_below = rank - first_row
        wide_out[start_row : start_row + rows_below] = jnp.broadcast_to(
            scaled[first_row:, r : r + 1], (rows_below, LANES)
        )

    for copy in ry_copies:
        copy.wait_recv()
    mttkrp = mine_x[reach]
    for d in range(1, ny):
        mttkrp = mttkrp + from_y[d]

    level_out[...] = columns_first(mttkrp - fitted) / pivot
    for copy in sent:
        copy.wait_send()


def sweep_kernel(wide, level_ref, out):
    rank, share = level_ref.shape[0], out.shape[0]
    level = level_ref[...]
    place = lax.broadcasted_iota(jnp.int32, (ROWS, LANES), 0)
    fresh = []
    for first_row in range(0, rank, ROWS):
        head, rest = level[:ROWS], level[ROWS:]
        done = head
        for k in range(ROWS):
            row = column_places(rank)[first_row + k][1]
            new = jnp.maximum(head, 0.0)
            done = jnp.where(place == k, new, done)
            column = jnp.broadcast_to(new[k : k + 1], (ROWS, LANES))
            if k < ROWS - 1:
                head = head - wide[row : row + ROWS] * column
            if rest.shape[0]:
                full = jnp.concatenate([column] * (rest.shape[0] // ROWS), axis=0)
                rest = rest - wide[row + ROWS : row + ROWS + rest.shape[0]] * full
        fresh.append(done)
        level = rest
    out[...] = jnp.concatenate(fresh, axis=0).T[:share]


def per_device(nu, ni, nt, blocks, block_coords, block_count, a_factor, item_factor, hour_factor):
    tiles = blocks.reshape(blocks.shape[3:])
    slots, width, depth = tiles.shape
    coords = jnp.transpose(block_coords, (0, 1, 4, 2, 3)).reshape(3, 1, slots)
    count = block_count.reshape((1, 1, 1))
    share, rank = a_factor.shape
    ri, rh = item_factor.shape[0], hour_factor.shape[0]
    ny = nt // 2
    strip_rows = rank // ny
    pieces = rh // ri
    wide_rows = sum(rank - first_row for first_row, _ in column_places(rank))
    hbm = pl.BlockSpec(memory_space=pltpu.MemorySpace.HBM)
    on_chip = pl.BlockSpec(memory_space=pltpu.VMEM)
    vmem, smem, dma = pltpu.VMEM, pltpu.SMEM, pltpu.SemaphoreType.DMA
    ready = pl.pallas_call(
        functools.partial(exchange_kernel, nu, ni, nt),
        out_shape=(vmem((wide_rows, LANES), F32), vmem((rank, LANES), F32)),
        in_specs=[hbm] * 6,
        out_specs=[on_chip] * 2,
        scratch_shapes=[
            smem((3, 1, slots), jnp.int32),
            smem((1, 1, 1), jnp.int32),
            vmem((share, rank), F32),
            vmem((nu, 1 + pieces, ri, rank), BF16),
            vmem((2, ny, nu, ri, rank), BF16),
            vmem((ni, nu, pieces, ri, rank), BF16),
            vmem((slots, width, depth), BF16),
            vmem((slots, width, rank), F32),
            vmem((2, ni, ny, share, rank), F32),
            vmem((ni, ny, share, rank), F32),
            vmem((ni, ny, share, rank), F32),
            vmem((ny, share, rank), F32),
            vmem((ny, share, rank), F32),
            vmem((2, rank, rank), F32),
            vmem((rank, rank), F32),
            vmem((ny, strip_rows, rank), F32),
            vmem((strip_rows, rank), F32),
            vmem((ni, strip_rows, rank), F32),
            vmem((strip_rows, rank), F32),
            vmem((strip_rows, rank), F32),
            vmem((rank, rank), F32),
            dma((4 + pieces,)),
            dma((slots,)),
            dma((nu,)), dma((nu,)),
            dma((ny,)), dma((ny,)), dma((2,)), dma((2,)), dma((ni,)), dma((ni,)),
            dma, dma, dma((ni,)), dma((ni,)), dma((ny,)), dma((ny,)), dma, dma, dma((ny,)), dma((ny,)),
            dma((2,)), dma((2,)), dma((2, ni)), dma((2, ni)), dma((ny,)), dma((ny,)),
        ],
        compiler_params=pltpu.CompilerParams(
            collective_id=0, has_side_effects=True, vmem_limit_bytes=54 * 1024 * 1024
        ),
        name="exchange",
    )(coords, count, tiles, a_factor, item_factor, hour_factor)
    return pl.pallas_call(
        sweep_kernel,
        out_shape=jax.ShapeDtypeStruct((share, rank), F32),
        in_specs=[on_chip] * 2,
        out_specs=on_chip,
        compiler_params=pltpu.CompilerParams(vmem_limit_bytes=8 * 1024 * 1024),
        name="sweep",
    )(*ready)


def solution(mesh):
    placed = (
        P("user", "item", "tm", None, None, None),
        P("user", "item", "tm", None, None),
        P("user", "item", "tm"),
        P(("user", "item", "tm"), None),
        P(("item", "user", "tm"), None),
        P(("tm", "user", "item"), None),
    )
    return jax.shard_map(
        functools.partial(per_device, mesh.shape["user"], mesh.shape["item"], mesh.shape["tm"]),
        mesh=mesh,
        in_specs=placed,
        out_specs=P(("user", "item", "tm"), None),
        check_vma=False,
    )
```

```python
import functools

import jax
import jax.numpy as jnp
from jax import lax
from jax.experimental import pallas as pl
from jax.experimental.pallas import tpu as pltpu
from jax.sharding import PartitionSpec as P

F32 = jnp.float32
BF16 = jnp.bfloat16
ROWS = 8
LANES = 128


def nearest_first(n):
    return sorted(range(1, n), key=lambda d: (min(d, n - d), d))


def farthest_first(n):
    return sorted(range(1, n), key=lambda d: (-min(d, n - d), d))


def self_product(rows):
    return lax.dot_general(rows, rows, (((0,), (0,)), ((), ())), preferred_element_type=F32)


def split(x, rows):
    return [x[k * rows : (k + 1) * rows] for k in range(x.shape[0] // rows)]


def column_places(rank):
    places, start = [], 0
    for r in range(rank):
        first_row = r // ROWS * ROWS
        places.append((first_row, start))
        start += rank - first_row
    return places


def columns_first(x):
    return jnp.concatenate([x] * (LANES // x.shape[0]), axis=0).T


def exchange_kernel(
    nu, ni, nt,
    coords_hbm, count_hbm, blocks, factor_hbm, item_hbm, hour_hbm,
    wide_out, level_out,
    coords, count, factor, rows_u, items, hours, tiles, terms, totals, from_core, from_x, mine_x, from_y,
    grams, g_core, g_y, g_sum, g_x, g_mine, g_other, gram,
    in_sem, tile_sem, z_send, z_recv, y_send, y_recv, c_send, c_recv, x_send, x_recv,
    gc_send, gc_recv, gx_send, gx_recv, gy_send, gy_recv, go_send, go_recv, ga_send, ga_recv,
    rc_send, rc_recv, rx_send, rx_recv, ry_send, ry_recv,
):
    ny = nt // 2
    u = lax.axis_index("user")
    i = lax.axis_index("item")
    t = lax.axis_index("tm")
    y, c = t // 2, t % 2
    slots, width, _ = tiles.shape
    ri, rh = item_hbm.shape[0], hour_hbm.shape[0]
    share, rank = factor.shape
    strip_rows = rank // ny
    pieces = rh // ri
    reach = ny // 4
    near = 2 * reach + 1

    def at_user(d):
        return {"user": (u + d) % nu}

    def at_item(d):
        return {"item": (i + d) % ni}

    def at_y(d):
        return {"tm": ((y + d) % ny) * 2 + c}

    def at_other(d):
        return {"tm": ((y + d) % ny) * 2 + 1 - c}

    sibling = at_other(0)

    def remote(src, dst, send, recv, device):
        return pltpu.make_async_remote_copy(
            src_ref=src, dst_ref=dst, send_sem=send, recv_sem=recv,
            device_id=device, device_id_type=pl.DeviceIdType.MESH,
        )

    def tile_copy(s):
        return pltpu.make_async_copy(blocks.at[s], tiles.at[s], tile_sem.at[s])

    own_rows = [pltpu.make_async_copy(item_hbm, rows_u.at[u, 0], in_sem.at[3])] + [
        pltpu.make_async_copy(hour_hbm.at[q * ri : (q + 1) * ri], rows_u.at[u, 1 + q], in_sem.at[4 + q])
        for q in range(pieces)
    ]
    later = [
        pltpu.make_async_copy(factor_hbm, factor, in_sem.at[0]),
        pltpu.make_async_copy(coords_hbm, coords, in_sem.at[1]),
        pltpu.make_async_copy(count_hbm, count, in_sem.at[2]),
    ]

    for copy in own_rows:
        copy.start()

    barrier = pltpu.get_barrier_semaphore()
    partners = (
        [at_user(d) for d in farthest_first(nu)]
        + [at_item(d) for d in farthest_first(ni)]
        + [at_y(d) for d in farthest_first(ny)]
        + [sibling]
    )
    for device in partners:
        pl.semaphore_signal(barrier, inc=1, device_id=device, device_id_type=pl.DeviceIdType.MESH)
    pl.semaphore_wait(barrier, len(partners))

    for copy in own_rows:
        copy.wait()
    sent = []

    def start(copy):
        copy.start()
        sent.append(copy)
        return copy

    for d in farthest_first(nu):
        start(remote(rows_u.at[u], rows_u.at[u], z_send.at[d], z_recv.at[u], at_user(d)))
    for copy in later:
        copy.start()
    for s in range(slots):
        tile_copy(s).start()
    for v in range(nu):
        pl.when(u != v)(remote(rows_u.at[v], rows_u.at[v], z_send.at[0], z_recv.at[v], at_user(1)).wait_recv)

    own_items, own_hours = rows_u.at[:, 0], rows_u.at[:, pl.ds(1, pieces)]
    y_copies = {
        d: start(remote(own_items, items.at[c, (reach + ny - d) % ny], y_send.at[d], y_recv.at[d], at_y(d)))
        for d in farthest_first(ny)
    }
    x_copies = [
        start(remote(own_hours, hours.at[i], x_send.at[d], x_recv.at[d], at_item(d))) for d in farthest_first(ni)
    ]
    items[c, reach] = own_items[...]
    hours[i] = own_hours[...]

    def strip(v):
        return pl.ds(pl.multiple_of(v * strip_rows, strip_rows), strip_rows)

    grams[0] = self_product(own_hours[...].reshape(nu * rh, rank))
    grams[1] = self_product(own_items[...].reshape(nu * ri, rank))
    gc_copy = start(remote(grams.at[1 - c], g_core, gc_send, gc_recv, sibling))
    gc_copy.wait_recv()
    grams[c] = grams[c] + g_core[...]
    gy_copies = [
        start(remote(grams.at[c, strip((y + d) % ny)], g_y.at[d], gy_send.at[d], gy_recv.at[d], at_y(d)))
        for d in farthest_first(ny)
    ]

    c_copies = []
    for k, part in enumerate([pl.ds(0, near), pl.ds(near, ny - near)]):
        for d in nearest_first(ny):
            if ((reach + ny - d) % ny >= near) == bool(k):
                y_copies[d].wait_recv()
        c_copies.append(start(remote(items.at[c, part], items.at[c, part], c_send.at[k], c_recv.at[k], sibling)))
    for copy in later:
        copy.wait()
    for copy in x_copies:
        copy.wait_recv()
    for copy in c_copies:
        copy.wait_recv()

    user_blocks = (share * ni * nt) // width
    item_blocks = (ri * nu * nt) // width
    hour_blocks = (rh * nu * ni) // width
    span = width // ri
    per_user = nt // span
    group = 16

    def product(s):
        tile_copy(s).wait()
        item_block = lax.rem(coords[1, 0, s], item_blocks)
        hour_block = lax.rem(coords[2, 0, s], hour_blocks)
        chip = lax.div(lax.rem(item_block, per_user) * span, 2) + ny - y + reach
        owner = lax.div(item_block, per_user)
        item_rows = [
            items[core, lax.rem(chip + step, ny), owner] for step in range(span // 2) for core in range(2)
        ]
        item_rows = jnp.concatenate([rows.astype(F32) for rows in item_rows], axis=0)
        hour_rows = hours[:, hour_block].astype(F32).reshape(width, rank)
        term = jnp.zeros((width, rank), F32)
        for g in range(width // group):
            khatri = jnp.concatenate(
                [(item_rows[j : j + 1, :] * hour_rows).astype(BF16) for j in range(g * group, (g + 1) * group)],
                axis=0,
            )
            part = tiles[s, :, g * group * width : (g + 1) * group * width]
            term = term + jnp.dot(part, khatri, preferred_element_type=F32)
        terms[s] = term

    pl.loop(0, slots // 2)(product)
    for copy in gy_copies:
        copy.wait_recv()
    g_total = grams[c, strip(y)]
    for d in range(1, ny):
        g_total = g_total + g_y[d]
    g_sum[...] = g_total
    gx_copies = [
        start(remote(g_sum, g_x.at[d], gx_send.at[d], gx_recv.at[d], at_item(d)))
        for d in farthest_first(ni)
    ]
    pl.loop(slots // 2, slots)(product)

    chunks = width // share

    @pl.loop(0, user_blocks)
    def _(b):
        total = jnp.zeros((width, rank), F32)
        for s in range(slots):
            block = jnp.where(s < count[0, 0, 0], lax.rem(coords[0, 0, s], user_blocks), -1)
            hit = jnp.full((width, rank), block, jnp.int32) == b
            total = total + jnp.where(hit, terms[s], 0.0)
        for q in range(chunks):
            chip = b * (chunks // 2) + q // 2
            place = (chip % ny + ny - y + reach) % ny
            totals[q % 2, chip // ny, place] = total[q * share : (q + 1) * share]

    parts = [pl.ds(near, ny - near), pl.ds(0, near)]
    rc_copies = [
        start(
            remote(
                totals.at[1 - c, :, part], from_core.at[:, part], rc_send.at[k], rc_recv.at[k], sibling
            )
        )
        for k, part in enumerate(parts)
    ]
    rx_copies = [[], []]
    for k, part in enumerate(parts):
        rc_copies[k].wait_recv()
        totals[c, :, part] = totals[c, :, part] + from_core[:, part]
        for d in farthest_first(ni):
            rx_copies[k].append(
                start(
                    remote(
                        totals.at[c, (i + d) % ni, part], from_x.at[d, part],
                        rx_send.at[k, d], rx_recv.at[k, d], at_item(d),
                    )
                )
            )
    for copy in gx_copies:
        copy.wait_recv()
    g_total = g_sum[...]
    for d in range(1, ni):
        g_total = g_total + g_x[d]
    g_mine[...] = g_total
    go_copy = start(remote(g_mine, g_other, go_send, go_recv, sibling))
    go_copy.wait_recv()
    gram[strip(y), :] = g_mine[...] * g_other[...]
    ga_copies = [
        start(remote(gram.at[strip(y)], gram.at[strip(y)], ga_send.at[d], ga_recv.at[d], at_y(d)))
        for d in farthest_first(ny)
    ]

    ry_copies = {}
    for k, part in enumerate(parts):
        for copy in rx_copies[k]:
            copy.wait_recv()
        summed = totals[c, i, part]
        for d in range(1, ni):
            summed = summed + from_x[d, part]
        mine_x[part] = summed
        for d in farthest_first(ny):
            place = (d + reach) % ny
            if (place >= near) == (k == 0):
                ry_copies[d] = start(
                    remote(mine_x.at[place], from_y.at[d], ry_send.at[d], ry_recv.at[d], at_y(d))
                )

    for copy in ga_copies:
        copy.wait_recv()
    weights = gram[...]
    current = factor[...]
    rows = lax.broadcasted_iota(jnp.int32, (rank, rank), 0)
    cols = lax.broadcasted_iota(jnp.int32, (rank, rank), 1)
    fitted = jnp.dot(
        current, jnp.where(rows > cols, weights, 0.0), precision=lax.Precision.HIGHEST, preferred_element_type=F32
    )
    pivot = jnp.sum(jnp.where(rows == cols, weights, 0.0), axis=1, keepdims=True)
    pivot = jnp.broadcast_to(pivot, (rank, LANES))
    scaled = weights / pivot
    for r, (first_row, start_row) in enumerate(column_places(rank)):
        rows_below = rank - first_row
        wide_out[start_row : start_row + rows_below] = jnp.broadcast_to(
            scaled[first_row:, r : r + 1], (rows_below, LANES)
        )

    mttkrp = mine_x[reach]
    for d in nearest_first(ny):
        ry_copies[d].wait_recv()
        mttkrp = mttkrp + from_y[d]

    level_out[...] = columns_first(mttkrp - fitted) / pivot
    for copy in sent:
        copy.wait_send()


def sweep_kernel(wide, level_ref, out):
    rank, share = level_ref.shape[0], out.shape[0]
    level = level_ref[...]
    place = lax.broadcasted_iota(jnp.int32, (ROWS, LANES), 0)
    fresh = []
    for first_row in range(0, rank, ROWS):
        head, rest = level[:ROWS], level[ROWS:]
        done = head
        for k in range(ROWS):
            row = column_places(rank)[first_row + k][1]
            new = jnp.maximum(head, 0.0)
            done = jnp.where(place == k, new, done)
            column = jnp.broadcast_to(new[k : k + 1], (ROWS, LANES))
            if k < ROWS - 1:
                head = head - wide[row : row + ROWS] * column
            if rest.shape[0]:
                full = jnp.concatenate([column] * (rest.shape[0] // ROWS), axis=0)
                rest = rest - wide[row + ROWS : row + ROWS + rest.shape[0]] * full
        fresh.append(done)
        level = rest
    out[...] = jnp.concatenate(fresh, axis=0).T[:share]


def per_device(nu, ni, nt, blocks, block_coords, block_count, a_factor, item_factor, hour_factor):
    tiles = blocks.reshape(blocks.shape[3:])
    slots, width, depth = tiles.shape
    coords = jnp.transpose(block_coords, (0, 1, 4, 2, 3)).reshape(3, 1, slots)
    count = block_count.reshape((1, 1, 1))
    share, rank = a_factor.shape
    ri, rh = item_factor.shape[0], hour_factor.shape[0]
    ny = nt // 2
    strip_rows = rank // ny
    pieces = rh // ri
    wide_rows = sum(rank - first_row for first_row, _ in column_places(rank))
    hbm = pl.BlockSpec(memory_space=pltpu.MemorySpace.HBM)
    on_chip = pl.BlockSpec(memory_space=pltpu.VMEM)
    vmem, smem, dma = pltpu.VMEM, pltpu.SMEM, pltpu.SemaphoreType.DMA
    ready = pl.pallas_call(
        functools.partial(exchange_kernel, nu, ni, nt),
        out_shape=(vmem((wide_rows, LANES), F32), vmem((rank, LANES), F32)),
        in_specs=[hbm] * 6,
        out_specs=[on_chip] * 2,
        scratch_shapes=[
            smem((3, 1, slots), jnp.int32),
            smem((1, 1, 1), jnp.int32),
            vmem((share, rank), F32),
            vmem((nu, 1 + pieces, ri, rank), BF16),
            vmem((2, ny, nu, ri, rank), BF16),
            vmem((ni, nu, pieces, ri, rank), BF16),
            vmem((slots, width, depth), BF16),
            vmem((slots, width, rank), F32),
            vmem((2, ni, ny, share, rank), F32),
            vmem((ni, ny, share, rank), F32),
            vmem((ni, ny, share, rank), F32),
            vmem((ny, share, rank), F32),
            vmem((ny, share, rank), F32),
            vmem((2, rank, rank), F32),
            vmem((rank, rank), F32),
            vmem((ny, strip_rows, rank), F32),
            vmem((strip_rows, rank), F32),
            vmem((ni, strip_rows, rank), F32),
            vmem((strip_rows, rank), F32),
            vmem((strip_rows, rank), F32),
            vmem((rank, rank), F32),
            dma((4 + pieces,)),
            dma((slots,)),
            dma((nu,)), dma((nu,)),
            dma((ny,)), dma((ny,)), dma((2,)), dma((2,)), dma((ni,)), dma((ni,)),
            dma, dma, dma((ni,)), dma((ni,)), dma((ny,)), dma((ny,)), dma, dma, dma((ny,)), dma((ny,)),
            dma((2,)), dma((2,)), dma((2, ni)), dma((2, ni)), dma((ny,)), dma((ny,)),
        ],
        compiler_params=pltpu.CompilerParams(
            collective_id=0, has_side_effects=True, vmem_limit_bytes=54 * 1024 * 1024
        ),
        name="exchange",
    )(coords, count, tiles, a_factor, item_factor, hour_factor)
    return pl.pallas_call(
        sweep_kernel,
        out_shape=jax.ShapeDtypeStruct((share, rank), F32),
        in_specs=[on_chip] * 2,
        out_specs=on_chip,
        compiler_params=pltpu.CompilerParams(vmem_limit_bytes=8 * 1024 * 1024),
        name="sweep",
    )(*ready)


def solution(mesh):
    placed = (
        P("user", "item", "tm", None, None, None),
        P("user", "item", "tm", None, None),
        P("user", "item", "tm"),
        P(("user", "item", "tm"), None),
        P(("item", "user", "tm"), None),
        P(("tm", "user", "item"), None),
    )
    return jax.shard_map(
        functools.partial(per_device, mesh.shape["user"], mesh.shape["item"], mesh.shape["tm"]),
        mesh=mesh,
        in_specs=placed,
        out_specs=P(("user", "item", "tm"), None),
        check_vma=False,
    )
```
